128 devices in a mesh: pix: 16 (over x, y), tm: 8 (over z, core).
Axes of the slice: x: 4, y: 4, z: 4, core: 2. Of those that a mesh axis runs over, the one named last changes fastest.
Arguments:
- raw_frames: float32 [1024, 131072], P(('tm', 'pix')), may hold values from 1 to 64
- frame_order: int32 [1024], P(('tm', 'pix')), may hold values from 0 to 7, as said below
- owner_map: int32 [1024], replicated, may hold values from 0 to 1023, each once
- pixel_mask: int32 [131072], replicated, may hold values 0 or 1
- dark: float32 [131072], replicated, may hold values from 0 to 0.5
- flat: float32 [131072], replicated, may hold values from 0.5 to 1.5
- polarization: float32 [131072], replicated, may hold values from 0.5 to 1
- solid_angle: float32 [131072], replicated, may hold values from 0.6 to 1
Outputs:
- g2: float32 [4, 16, 131072], P(None, None, ('pix', 'tm'))
- mean_frame: float32 [131072], P(('pix', 'tm'))
The draws below stay inside these ranges and needn't reach their ends.
Inputs may be any that keep to these rules, and one draw needn't show every extreme that they name: `frame_order`: each aligned block of 8 entries is a permutation of 0 .. 7. `owner_map`: a permutation of the block numbers.
All inputs are finite; a program needn't handle non-finite values.
Results may differ from the reference program's by a relative error of at most 0.0003.
Values sent between devices are 32-bit elements; how exact they have to be, the bound alone decides.
A program may use at most 128 MiB of HBM per device.

```python
import math
import jax
import jax.numpy as jnp
from jax import lax

FRAMES = 1024
LAGS = 16
LEVELS = 4
BLK = 128
PIX_DEV = 8192
NPIX = 131072
NBLK = 1024
READ = 8
N_PIX = 16
N_TM = 8


def draw_frame_order(key, part):
    block_keys = jax.random.split(jax.random.fold_in(key, 17), FRAMES // READ)
    shuffled = jax.vmap(lambda one_key: jax.random.permutation(one_key, READ))(block_keys)
    return shuffled.reshape(FRAMES).astype(jnp.int32)


def place_ends(drawn, stream_key, least, high):
    index_at = [jax.random.randint(jax.random.fold_in(stream_key, axis), (), 0, length) for axis, length in enumerate(drawn.shape)]
    main_axis = drawn.shape.index(max(drawn.shape))
    next_to = index_at[:main_axis] + [(index_at[main_axis] + 1) % drawn.shape[main_axis]] + index_at[main_axis + 1:]
    return drawn.at[tuple(index_at)].set(least).at[tuple(next_to)].set(high)


def block_levels(rng, shape, shards, smallest, top_value):
    def one(position, parts):
        heights = jax.random.uniform(jax.random.fold_in(jax.random.fold_in(rng, 6), position), (parts,), jnp.float32, smallest / len(shards), top_value / len(shards))
        return jnp.repeat(jnp.exp(heights), shape[position] // parts).reshape((-1,) + (1,) * (len(shape) - position - 1))

    level = one(*shards[0])
    for cut in shards[1:]:
        level = level * one(*cut)
    return level


def setup_inputs(seed: int = 0) -> dict:
    key_of = jax.random.split(jax.random.key(seed), 9)
    return {
        "raw_frames": jnp.clip(jnp.exp(math.log(64.0) - 4.158883 * jax.random.uniform(key_of[0], (FRAMES, NPIX), jnp.float32) ** block_levels(key_of[0], (FRAMES, NPIX), ((0, 128),), -0.2, 0.2)), 1.0, 64.0),
        "frame_order": draw_frame_order(jax.random.fold_in(key_of[8], 71), 0),
        "owner_map": jax.random.permutation(key_of[2], NBLK).astype(jnp.int32),
        "pixel_mask": place_ends((jax.random.randint(key_of[3], (NPIX,), 0, 10) < 9).astype(jnp.int32), jax.random.fold_in(key_of[3], 1), 0, 1),
        "dark": jnp.clip(jax.random.uniform(key_of[4], (NPIX,), jnp.float32, 0.0, 0.5), 0.0, 0.5),
        "flat": jnp.clip(1.0 + 0.1 * jax.random.normal(key_of[5], (NPIX,), jnp.float32), 0.5, 1.5),
        "polarization": jnp.clip(jax.random.uniform(key_of[6], (NPIX,), jnp.float32, 0.5, 1.0), 0.5, 1.0),
        "solid_angle": jnp.clip(jax.random.uniform(key_of[7], (NPIX,), jnp.float32, 0.6, 1.0), 0.6, 1.0),
    }


def coarsen(series):
    pairs = series.reshape(series.shape[0] // 2, 2, series.shape[1])
    return 0.5 * (pairs[:, 0] + pairs[:, 1])


def reference(raw_frames, frame_order, owner_map, pixel_mask, dark, flat, polarization, solid_angle):
    read_len = FRAMES // (N_TM * N_PIX)
    rows_idx = (jnp.arange(FRAMES, dtype=jnp.int32) // read_len) * read_len + frame_order.astype(jnp.int32)
    timed = jnp.take(raw_frames, rows_idx, axis=0)
    source = (owner_map[:, None].astype(jnp.int32) * BLK + jnp.arange(BLK, dtype=jnp.int32)[None, :]).reshape(NPIX)
    response = flat * polarization * solid_angle

    def one_group(group_no):
        picked = lax.dynamic_slice_in_dim(source, (group_no * PIX_DEV).astype(jnp.int32), PIX_DEV)
        block_data = jnp.take(timed, picked, axis=1)
        corrected = (block_data - jnp.take(dark, picked)) / jnp.take(response, picked)
        mean_raw = jnp.sum(corrected, axis=0) / FRAMES
        keeper = jnp.take(pixel_mask, picked).astype(jnp.float32)
        series = corrected
        results = []
        for level_no in range(LEVELS):
            length = FRAMES >> level_no
            products = []
            for lag_no in range(1, LAGS + 1):
                products.append(jnp.sum(series[:length - lag_no] * series[lag_no:], axis=0))
            product = jnp.stack(products)
            counts = (length - jnp.arange(1, LAGS + 1, dtype=jnp.int32)).astype(jnp.float32)[:, None]
            results.append(product / (counts * mean_raw * mean_raw) * keeper)
            if level_no + 1 < LEVELS:
                series = coarsen(series)
        return jnp.stack(results), mean_raw * keeper

    corr_all, means_all = lax.map(one_group, jnp.arange(NPIX // PIX_DEV, dtype=jnp.int32))
    g2 = jnp.transpose(corr_all, (1, 2, 0, 3)).reshape(LEVELS, LAGS, NPIX)
    return g2, means_all.reshape(NPIX)
```

```python
import jax
import jax.numpy as jnp
from jax import lax
from jax.experimental import pallas as pl
from jax.experimental.pallas import tpu as pltpu
from jax.sharding import PartitionSpec as P

FRAMES = 1024
LAGS = 16
LEVELS = 4
READ = 8
BLK = 128
N_PIX = 16
N_TM = 8
SIDE = 4
N_DEV = N_PIX * N_TM
SEG = FRAMES // N_TM
GROUP = 4
MESH = pl.DeviceIdType.MESH


def step_offset(phase):
    return ((phase + 1) // 2) * (2 * (phase % 2) - 1)


def step_target(step, pix, tm):
    phase, turn = step // N_PIX, step % N_PIX
    to_x = (pix // SIDE + turn % SIDE) % SIDE
    to_y = (pix % SIDE + turn // SIDE) % SIDE
    to_tm = (tm - step_offset(phase) + N_TM) % N_TM
    return to_x * SIDE + to_y, to_tm


def lag_group(fresh, before, sums):
    rows = before + fresh
    sums = list(sums)
    for i in range(LAGS):
        for lag in range(1, LAGS + 1):
            sums[lag - 1] = sums[lag - 1] + fresh[i] * rows[LAGS + i - lag]
    return sums


def stage_kernel(owner, order, raw_in, dark_in, flat_in, pol_in, solid_in, mask_in, staged, consts,
                 raw_v, tmp, stage, rows_v, mask_v, load_sem, row_sem, mask_sem, out_sem):
    pix = lax.axis_index("pix")
    tm = lax.axis_index("tm")
    me = pix * N_TM + tm

    load = pltpu.make_async_copy(raw_in, raw_v, load_sem)
    load.start()
    for j in range(8):
        block = owner[me * 8 + j]
        for i, src in enumerate((dark_in, flat_in, pol_in, solid_in)):
            pltpu.make_async_copy(src.at[pl.ds(block, 1)], rows_v.at[i, pl.ds(j, 1)], row_sem).start()
        pltpu.make_async_copy(mask_in.at[pl.ds(block, 1)], mask_v.at[pl.ds(j, 1)], mask_sem).start()
    load.wait()

    def put(turn, carry):
        step0 = turn * GROUP
        for u in range(GROUP):
            to_pix, to_tm = step_target(step0 + u, pix, tm)
            base = (to_pix * N_TM + to_tm) * 8
            for j in range(8):
                block = owner[base + j]
                tmp[u, pl.ds(j, 8, stride=8), :] = raw_v[:, pl.ds(pl.multiple_of(block * BLK, BLK), BLK)]
        for u in range(GROUP):
            for r in range(READ):
                stage[step0 + u, r] = tmp[u, pl.ds(pl.multiple_of(order[r] * 8, 8), 8), :]
        part = pl.ds(step0, GROUP)
        pltpu.make_async_copy(stage.at[part], staged.at[part], out_sem).start()
        return carry

    lax.fori_loop(0, N_DEV // GROUP, put, 0)
    pltpu.make_async_copy(rows_v, rows_v, row_sem).wait()
    pltpu.make_async_copy(mask_v, mask_v, mask_sem).wait()
    consts[0] = rows_v[0]
    consts[1] = rows_v[1] * rows_v[2] * rows_v[3]
    consts[2] = mask_v[...].astype(jnp.float32)
    pltpu.make_async_copy(stage, stage, out_sem).wait()


def kernel(staged, consts, g2_out, mean_out, tmp, xs, s1, s2, s3, sums, own_sem, send_sem, recv_sem):
    pix = lax.axis_index("pix")
    tm = lax.axis_index("tm")
    barrier = pltpu.get_barrier_semaphore()

    def greet(step, carry):
        to_pix, to_tm = step_target(step, pix, tm)
        pl.semaphore_signal(barrier, inc=1, device_id={"pix": to_pix, "tm": to_tm}, device_id_type=MESH)
        return carry

    lax.fori_loop(1, N_DEV, greet, 0)

    zero = jnp.zeros((8, BLK), jnp.float32)
    for buf in (xs, s1, s2, s3):
        for i in range(LAGS):
            buf[i] = zero
    for level in range(LEVELS):
        for lag in range(LAGS):
            sums[level, lag] = zero
    dark = consts[0]
    inverse = 1.0 / consts[1]

    my_rows = xs.at[pl.ds(LAGS + tm * SEG + pix * READ, READ)]

    def send(step, carry):
        to_pix, to_tm = step_target(step, pix, tm)
        pltpu.make_async_remote_copy(
            src_ref=staged.at[step],
            dst_ref=my_rows,
            send_sem=send_sem,
            recv_sem=recv_sem.at[tm],
            device_id={"pix": to_pix, "tm": to_tm},
            device_id_type=MESH,
        ).start()
        return carry

    own = pltpu.make_async_copy(staged.at[0], my_rows, own_sem)
    own.start()
    pl.semaphore_wait(barrier, N_DEV - 1)
    lax.fori_loop(1, N_DEV, send, 0)
    own.wait()

    def level_pass(level, buf, deeper, seg, joined):
        rows = SEG >> level
        first = LAGS + seg * rows

        def group(g, acc):
            start = first + g * LAGS
            fresh = [buf[start + i] for i in range(LAGS)]
            if level == 0:
                fresh = [(one - dark) * inverse for one in fresh]
                for i in range(LAGS):
                    buf[start + i] = fresh[i]
            back = jnp.where((g > 0) | joined, start - LAGS, 0)
            before = [buf[back + i] for i in range(LAGS)]
            if deeper is not None:
                for i in range(LAGS // 2):
                    deeper[LAGS + (seg * rows + g * LAGS) // 2 + i] = 0.5 * (fresh[2 * i] + fresh[2 * i + 1])
            return tuple(lag_group(fresh, before, acc))

        acc = tuple(sums[level, lag] for lag in range(LAGS))
        acc = lax.fori_loop(0, rows // LAGS, group, acc)
        for lag in range(LAGS):
            sums[level, lag] = acc[lag]

    def border(seg):
        for level, buf in enumerate((xs, s1, s2, s3)):
            first = LAGS + seg * (SEG >> level)
            rows = [buf[first - LAGS + i] for i in range(2 * LAGS)]
            for lag in range(1, LAGS + 1):
                part = sums[level, lag - 1]
                for i in range(lag):
                    part = part + rows[LAGS + i] * rows[LAGS + i - lag]
                sums[level, lag - 1] = part

    def segment(phase, carry):
        offset = step_offset(phase)
        seg = (tm + offset + N_TM) % N_TM

        @pl.when(phase == 0)
        def _():
            part = xs.at[pl.ds(LAGS, (N_PIX - 1) * READ)]
            pltpu.make_async_copy(part, part, recv_sem.at[seg]).wait()

        @pl.when(phase > 0)
        def _():
            part = xs.at[pl.ds(LAGS, N_PIX * READ)]
            pltpu.make_async_copy(part, part, recv_sem.at[seg]).wait()

        joined = (offset > 0) & (seg > 0)
        for level, (buf, deeper) in enumerate(((xs, s1), (s1, s2), (s2, s3), (s3, None))):
            level_pass(level, buf, deeper, seg, joined)
        after = (seg + 1) % N_TM

        @pl.when(((offset < 0) | (phase == N_TM - 1)) & (after > 0))
        def _():
            border(after)

        return carry

    lax.fori_loop(0, N_TM, segment, 0)

    total = s3[LAGS]
    for i in range(1, FRAMES >> 3):
        total = total + s3[LAGS + i]
    mean = total / (FRAMES >> 3)
    keeper = consts[2]
    scale = keeper / (mean * mean)
    shown = mean * keeper
    mean_out[...] = shown
    flat_sums = tmp
    for level in range(LEVELS):
        for half in range(2):
            for k in range(8):
                lag = half * 8 + k
                flat_sums[half, pl.ds(k * 8, 8), :] = sums[level, lag] * (scale * (1.0 / ((FRAMES >> level) - lag - 1)))
            for j in range(8):
                g2_out[level, pl.ds(half * 8, 8), pl.ds(j * BLK, BLK)] = flat_sums[half, pl.ds(j, 8, stride=8), :]

    sent = xs.at[pl.ds(LAGS, (N_DEV - 1) * READ)]
    pltpu.make_async_copy(sent, sent, send_sem).wait()


def body(raw_frames, frame_order, owner_map, pixel_mask, dark, flat, polarization, solid_angle):
    n_blocks = owner_map.shape[0]
    tiles = [a.reshape(n_blocks, BLK) for a in (dark, flat, polarization, solid_angle, pixel_mask)]
    hbm = pl.BlockSpec(memory_space=pl.ANY)
    smem = pl.BlockSpec(memory_space=pltpu.SMEM)
    vmem = pl.BlockSpec(memory_space=pltpu.VMEM)
    f32 = jnp.float32
    staged, consts = pl.pallas_call(
        stage_kernel,
        out_shape=(
            jax.ShapeDtypeStruct((N_DEV, READ, 8, BLK), f32),
            jax.ShapeDtypeStruct((3, 8, BLK), f32),
        ),
        in_specs=[smem, smem] + [hbm] * 6,
        out_specs=(hbm, vmem),
        scratch_shapes=[
            pltpu.VMEM(raw_frames.shape, f32),
            pltpu.VMEM((GROUP, 64, BLK), f32),
            pltpu.VMEM((N_DEV, READ, 8, BLK), f32),
            pltpu.VMEM((4, 8, BLK), f32),
            pltpu.VMEM((8, BLK), jnp.int32),
            pltpu.SemaphoreType.DMA,
            pltpu.SemaphoreType.DMA,
            pltpu.SemaphoreType.DMA,
            pltpu.SemaphoreType.DMA,
        ],
    )(owner_map, frame_order, raw_frames, *tiles)
    g2, mean = pl.pallas_call(
        kernel,
        out_shape=(
            jax.ShapeDtypeStruct((LEVELS, LAGS, 8 * BLK), f32),
            jax.ShapeDtypeStruct((8, BLK), f32),
        ),
        in_specs=[hbm, vmem],
        out_specs=(vmem, vmem),
        scratch_shapes=[
            pltpu.VMEM((2, 64, BLK), f32),
            pltpu.VMEM((LAGS + FRAMES, 8, BLK), f32),
            pltpu.VMEM((LAGS + FRAMES // 2, 8, BLK), f32),
            pltpu.VMEM((LAGS + FRAMES // 4, 8, BLK), f32),
            pltpu.VMEM((LAGS + FRAMES // 8, 8, BLK), f32),
            pltpu.VMEM((LEVELS, LAGS, 8, BLK), f32),
            pltpu.SemaphoreType.DMA,
            pltpu.SemaphoreType.DMA,
            pltpu.SemaphoreType.DMA((N_TM,)),
        ],
        compiler_params=pltpu.CompilerParams(collective_id=0, has_side_effects=True),
    )(staged, consts)
    return g2, mean.reshape(8 * BLK)


def solution(mesh):
    return jax.shard_map(
        body,
        mesh=mesh,
        in_specs=(P(("tm", "pix"), None), P(("tm", "pix")), P(), P(), P(), P(), P(), P()),
        out_specs=(P(None, None, ("pix", "tm")), P(("pix", "tm"))),
        check_vma=False,
    )
```

```python
import jax
import jax.numpy as jnp
from jax import lax
from jax.experimental import pallas as pl
from jax.experimental.pallas import tpu as pltpu
from jax.sharding import PartitionSpec as P

FRAMES = 1024
LAGS = 16
LEVELS = 4
READ = 8
BLK = 128
N_PIX = 16
N_TM = 8
SIDE = 4
N_DEV = N_PIX * N_TM
SEG = FRAMES // N_TM
GROUP = 4
MESH = pl.DeviceIdType.MESH


ORDER = (0, 4, 1, -1, 3, -3, 2, -2)


def pick(table, index):
    value = table[0]
    for i, entry in enumerate(table[1:], 1):
        value = jnp.where(index == i, entry, value)
    return value


def before_done(phase, side):
    return int(any((ORDER[phase] + side - done) % N_TM == 0 for done in ORDER[:phase]))


def step_target(step, pix, tm):
    turn = lax.rem(step, 32)
    at = lax.div(turn, 2)
    offset = pick(ORDER, lax.div(step, 32) * 2 + lax.rem(turn, 2))
    x, y = lax.div(pix, SIDE), lax.rem(pix, SIDE)
    to_x = lax.rem(x + at, SIDE)
    to_y = lax.rem(y + at + lax.div(at, SIDE), SIDE)
    return to_x * SIDE + to_y, lax.rem(tm - offset + N_TM, N_TM)


def lag_group(fresh, before, sums):
    rows = before + fresh
    sums = list(sums)
    for i in range(LAGS):
        for lag in range(1, LAGS + 1):
            sums[lag - 1] = sums[lag - 1] + fresh[i] * rows[LAGS + i - lag]
    return sums


def kernel(owner, order, raw_in, dark_in, flat_in, pol_in, solid_in, mask_in, g2_out, mean_out,
           raw_v, tmp, stage, xs, s1, s2, s3, sums, consts, dark_v, flat_v, pol_v, solid_v, mask_v,
           load_sem, const_sem, own_sem, send_sem, recv_sem):
    pix = lax.axis_index("pix")
    tm = lax.axis_index("tm")
    me = pix * N_TM + tm

    load = pltpu.make_async_copy(raw_in, raw_v, load_sem)
    load.start()

    barrier = pltpu.get_barrier_semaphore()

    def greet(step, carry):
        to = lax.rem(me + step, N_DEV)
        peer = {"pix": lax.div(to, N_TM), "tm": lax.rem(to, N_TM)}
        pl.semaphore_signal(barrier, inc=1, device_id=peer, device_id_type=MESH)
        return carry

    lax.fori_loop(1, N_DEV, greet, 0)

    const_copies = [
        pltpu.make_async_copy(src, dst, const_sem.at[i])
        for i, (src, dst) in enumerate(
            ((dark_in, dark_v), (flat_in, flat_v), (pol_in, pol_v), (solid_in, solid_v), (mask_in, mask_v))
        )
    ]
    for copy in const_copies:
        copy.start()

    zero = jnp.zeros((8, BLK), jnp.float32)
    for buf in (xs, s1, s2, s3):
        for i in range(LAGS):
            buf[i] = zero
    for level in range(LEVELS):
        for lag in range(LAGS):
            sums[level, lag] = zero
    load.wait()
    rows_tmp = tmp.reshape(GROUP, 64, BLK)

    def put(turn, carry):
        for u in range(GROUP):
            to = turn * GROUP + u
            for j in range(8):
                rows_tmp[u, pl.ds(j, 8, stride=8), :] = raw_v[owner[to * 8 + j]]
        for u in range(GROUP):
            for r in range(READ):
                stage[turn * GROUP + u, r] = tmp[u, order[r]]
        return carry

    lax.fori_loop(0, N_DEV // GROUP, put, 0)

    for copy in const_copies:
        copy.wait()
    for j in range(8):
        block = owner[me * 8 + j]
        consts[0, j] = dark_v[block]
        consts[1, j] = flat_v[block] * pol_v[block] * solid_v[block]
        consts[2, j] = mask_v[block].astype(jnp.float32)
    dark = consts[0]
    inverse = 1.0 / consts[1]

    my_rows = xs.at[pl.ds(LAGS + tm * SEG + pix * READ, READ)]

    def send(step, carry):
        to_pix, to_tm = step_target(step, pix, tm)
        pltpu.make_async_remote_copy(
            src_ref=stage.at[to_pix * N_TM + to_tm],
            dst_ref=my_rows,
            send_sem=send_sem,
            recv_sem=recv_sem.at[tm],
            device_id={"pix": to_pix, "tm": to_tm},
            device_id_type=MESH,
        ).start()
        return carry

    own = pltpu.make_async_copy(stage.at[me], my_rows, own_sem)
    own.start()
    pl.semaphore_wait(barrier, N_DEV - 1)
    lax.fori_loop(1, N_DEV, send, 0)
    own.wait()

    def level_pass(level, buf, deeper, seg, joined):
        rows = SEG >> level
        first = LAGS + seg * rows

        def group(g, acc):
            start = first + g * LAGS
            fresh = [buf[start + i] for i in range(LAGS)]
            if level == 0:
                fresh = [(one - dark) * inverse for one in fresh]
                for i in range(LAGS):
                    buf[start + i] = fresh[i]
            back = jnp.where((g > 0) | joined, start - LAGS, 0)
            before = [buf[back + i] for i in range(LAGS)]
            if deeper is not None:
                for i in range(LAGS // 2):
                    deeper[LAGS + (seg * rows + g * LAGS) // 2 + i] = 0.5 * (fresh[2 * i] + fresh[2 * i + 1])
            return tuple(lag_group(fresh, before, acc))

        acc = tuple(sums[level, lag] for lag in range(LAGS))
        acc = lax.fori_loop(0, rows // LAGS, group, acc)
        for lag in range(LAGS):
            sums[level, lag] = acc[lag]

    def border(seg):
        for level, buf in enumerate((xs, s1, s2, s3)):
            first = LAGS + seg * (SEG >> level)
            rows = [buf[first - LAGS + i] for i in range(2 * LAGS)]
            for lag in range(1, LAGS + 1):
                part = sums[level, lag - 1]
                for i in range(lag):
                    part = part + rows[LAGS + i] * rows[LAGS + i - lag]
                sums[level, lag - 1] = part

    def segment(phase, carry):
        seg = lax.rem(tm + pick(ORDER, phase) + N_TM, N_TM)

        @pl.when(phase == 0)
        def _():
            part = xs.at[pl.ds(LAGS, (N_PIX - 1) * READ)]
            pltpu.make_async_copy(part, part, recv_sem.at[seg]).wait()

        @pl.when(phase > 0)
        def _():
            part = xs.at[pl.ds(LAGS, N_PIX * READ)]
            pltpu.make_async_copy(part, part, recv_sem.at[seg]).wait()

        joined = (pick([before_done(i, -1) for i in range(N_TM)], phase) > 0) & (seg > 0)
        for level, (buf, deeper) in enumerate(((xs, s1), (s1, s2), (s2, s3), (s3, None))):
            level_pass(level, buf, deeper, seg, joined)
        after = lax.rem(seg + 1, N_TM)

        @pl.when((pick([before_done(i, 1) for i in range(N_TM)], phase) > 0) & (after > 0))
        def _():
            border(after)

        return carry

    lax.fori_loop(0, N_TM, segment, 0)

    total = s3[LAGS]
    for i in range(1, FRAMES >> 3):
        total = total + s3[LAGS + i]
    mean = total / (FRAMES >> 3)
    keeper = consts[2]
    scale = keeper / (mean * mean)
    shown = mean * keeper
    mean_out[...] = shown
    flat_sums = rows_tmp
    for level in range(LEVELS):
        for half in range(2):
            for k in range(8):
                lag = half * 8 + k
                flat_sums[half, pl.ds(k * 8, 8), :] = sums[level, lag] * (scale * (1.0 / ((FRAMES >> level) - lag - 1)))
            for j in range(8):
                g2_out[level, pl.ds(half * 8, 8), pl.ds(j * BLK, BLK)] = flat_sums[half, pl.ds(j, 8, stride=8), :]

    sent = xs.at[pl.ds(LAGS, (N_DEV - 1) * READ)]
    pltpu.make_async_copy(sent, sent, send_sem).wait()


def body(raw_frames, frame_order, owner_map, pixel_mask, dark, flat, polarization, solid_angle):
    n_blocks = owner_map.shape[0]
    tiles = [a.reshape(n_blocks, BLK) for a in (dark, flat, polarization, solid_angle, pixel_mask)]
    hbm = pl.BlockSpec(memory_space=pl.ANY)
    smem = pl.BlockSpec(memory_space=pltpu.SMEM)
    vmem = pl.BlockSpec(memory_space=pltpu.VMEM)
    f32 = jnp.float32
    blocks = raw_frames.reshape(READ, n_blocks, BLK).transpose(1, 0, 2)
    g2, mean = pl.pallas_call(
        kernel,
        out_shape=(
            jax.ShapeDtypeStruct((LEVELS, LAGS, 8 * BLK), f32),
            jax.ShapeDtypeStruct((8, BLK), f32),
        ),
        in_specs=[smem, smem] + [hbm] * 6,
        out_specs=(vmem, vmem),
        scratch_shapes=[
            pltpu.VMEM(blocks.shape, f32),
            pltpu.VMEM((GROUP, 8, 8, BLK), f32),
            pltpu.VMEM((N_DEV, READ, 8, BLK), f32),
            pltpu.VMEM((LAGS + FRAMES, 8, BLK), f32),
            pltpu.VMEM((LAGS + FRAMES // 2, 8, BLK), f32),
            pltpu.VMEM((LAGS + FRAMES // 4, 8, BLK), f32),
            pltpu.VMEM((LAGS + FRAMES // 8, 8, BLK), f32),
            pltpu.VMEM((LEVELS, LAGS, 8, BLK), f32),
            pltpu.VMEM((3, 8, BLK), f32),
        ]
        + [pltpu.VMEM((n_blocks, BLK), f32)] * 4
        + [
            pltpu.VMEM((n_blocks, BLK), jnp.int32),
            pltpu.SemaphoreType.DMA,
            pltpu.SemaphoreType.DMA((5,)),
            pltpu.SemaphoreType.DMA,
            pltpu.SemaphoreType.DMA,
            pltpu.SemaphoreType.DMA((N_TM,)),
        ],
        compiler_params=pltpu.CompilerParams(collective_id=0, has_side_effects=True),
    )(owner_map, frame_order, blocks, *tiles)
    return g2, mean.reshape(8 * BLK)


def solution(mesh):
    return jax.shard_map(
        body,
        mesh=mesh,
        in_specs=(P(("tm", "pix"), None), P(("tm", "pix")), P(), P(), P(), P(), P(), P()),
        out_specs=(P(None, None, ("pix", "tm")), P(("pix", "tm"))),
        check_vma=False,
    )
```

```python
import jax
import jax.numpy as jnp
from jax import lax
from jax.experimental import pallas as pl
from jax.experimental.pallas import tpu as pltpu
from jax.sharding import PartitionSpec as P

FRAMES = 1024
LAGS = 16
LEVELS = 4
READ = 8
BLK = 128
N_PIX = 16
N_TM = 8
SIDE = 4
N_DEV = N_PIX * N_TM
SEG = FRAMES // N_TM
GROUP = 4
MESH = pl.DeviceIdType.MESH


ORDER = (0, 4, 1, -1, 3, -3, 2, -2)


def pick(table, index):
    value = table[0]
    for i, entry in enumerate(table[1:], 1):
        value = jnp.where(index == i, entry, value)
    return value


def before_done(phase, side):
    return int(any((ORDER[phase] + side - done) % N_TM == 0 for done in ORDER[:phase]))


def step_target(step, pix, tm):
    core = lax.rem(tm, 2)
    turn = lax.rem(step, 32)
    offset = pick(ORDER, lax.div(step, 32) * 2 + lax.rem(turn + core, 2))
    at = lax.div(turn, 2) + 8 * core
    to_x = lax.rem(lax.div(pix, SIDE) + at, SIDE)
    to_y = lax.rem(lax.rem(pix, SIDE) + at + lax.div(at, SIDE), SIDE)
    return to_x * SIDE + to_y, lax.rem(tm - offset + N_TM, N_TM)


def lag_group(fresh, before, sums):
    rows = before + fresh
    sums = list(sums)
    for i in range(LAGS):
        for lag in range(1, LAGS + 1):
            sums[lag - 1] = sums[lag - 1] + fresh[i] * rows[LAGS + i - lag]
    return sums


def kernel(owner_in, order_in, raw_in, dark_in, flat_in, pol_in, solid_in, mask_in, sums, ends,
           raw_v, tmp, stage, xs, s1, s2, s3, consts, dark_v, flat_v, pol_v, solid_v, mask_v,
           owner, order, load_sem, map_sem, const_sem, own_sem, send_sem, recv_sem):
    pix = lax.axis_index("pix")
    tm = lax.axis_index("tm")
    me = pix * N_TM + tm

    load = pltpu.make_async_copy(raw_in, raw_v, load_sem)
    load.start()
    maps = [
        pltpu.make_async_copy(owner_in, owner, map_sem.at[0]),
        pltpu.make_async_copy(order_in, order, map_sem.at[1]),
    ]
    for copy in maps:
        copy.start()

    barrier = pltpu.get_barrier_semaphore()

    def greet(step, carry):
        to = lax.rem(me + step, N_DEV)
        peer = {"pix": lax.div(to, N_TM), "tm": lax.rem(to, N_TM)}
        pl.semaphore_signal(barrier, inc=1, device_id=peer, device_id_type=MESH)
        return carry

    lax.fori_loop(1, N_DEV, greet, 0)

    const_copies = [
        pltpu.make_async_copy(src, dst, const_sem.at[i])
        for i, (src, dst) in enumerate(
            ((dark_in, dark_v), (flat_in, flat_v), (pol_in, pol_v), (solid_in, solid_v), (mask_in, mask_v))
        )
    ]
    for copy in const_copies:
        copy.start()

    zero = jnp.zeros((8, BLK), jnp.float32)
    for buf in (xs, s1, s2, s3):
        for i in range(LAGS):
            buf[i] = zero
    for level in range(LEVELS):
        for lag in range(LAGS):
            sums[level, lag] = zero
    load.wait()
    for copy in maps:
        copy.wait()
    rows_tmp = tmp.reshape(GROUP, 64, BLK)

    def put(turn, carry):
        for u in range(GROUP):
            to = turn * GROUP + u
            for j in range(8):
                rows_tmp[u, pl.ds(j, 8, stride=8), :] = raw_v[owner[to * 8 + j]]
        for u in range(GROUP):
            for r in range(READ):
                stage[turn * GROUP + u, r] = tmp[u, order[r]]
        return carry

    lax.fori_loop(0, N_DEV // GROUP, put, 0)

    for copy in const_copies:
        copy.wait()
    for j in range(8):
        block = owner[me * 8 + j]
        consts[0, j] = dark_v[block]
        consts[1, j] = flat_v[block] * pol_v[block] * solid_v[block]
        consts[2, j] = mask_v[block].astype(jnp.float32)
    dark = consts[0]
    inverse = 1.0 / consts[1]

    my_rows = xs.at[pl.ds(LAGS + tm * SEG + pix * READ, READ)]

    def send(step, carry):
        to_pix, to_tm = step_target(step, pix, tm)
        to = to_pix * N_TM + to_tm

        @pl.when(to != me)
        def _():
            pltpu.make_async_remote_copy(
                src_ref=stage.at[to],
                dst_ref=my_rows,
                send_sem=send_sem,
                recv_sem=recv_sem.at[tm],
                device_id={"pix": to_pix, "tm": to_tm},
                device_id_type=MESH,
            ).start()

        return carry

    own = pltpu.make_async_copy(stage.at[me], my_rows, own_sem)
    own.start()
    pl.semaphore_wait(barrier, N_DEV - 1)
    lax.fori_loop(0, N_DEV, send, 0)
    own.wait()

    def level_pass(level, buf, deeper, seg, joined):
        rows = SEG >> level
        first = LAGS + seg * rows

        def group(g, acc):
            start = first + g * LAGS
            fresh = [buf[start + i] for i in range(LAGS)]
            if level == 0:
                fresh = [(one - dark) * inverse for one in fresh]
                for i in range(LAGS):
                    buf[start + i] = fresh[i]
            back = jnp.where((g > 0) | joined, start - LAGS, 0)
            before = [buf[back + i] for i in range(LAGS)]
            if deeper is not None:
                for i in range(LAGS // 2):
                    deeper[LAGS + (seg * rows + g * LAGS) // 2 + i] = 0.5 * (fresh[2 * i] + fresh[2 * i + 1])
            return tuple(lag_group(fresh, before, acc))

        acc = tuple(sums[level, lag] for lag in range(LAGS))
        acc = lax.fori_loop(0, rows // LAGS, group, acc)
        for lag in range(LAGS):
            sums[level, lag] = acc[lag]

    def border(seg):
        for level, buf in enumerate((xs, s1, s2, s3)):
            first = LAGS + seg * (SEG >> level)
            rows = [buf[first - LAGS + i] for i in range(2 * LAGS)]
            for lag in range(1, LAGS + 1):
                part = sums[level, lag - 1]
                for i in range(lag):
                    part = part + rows[LAGS + i] * rows[LAGS + i - lag]
                sums[level, lag - 1] = part

    def segment(phase, carry):
        seg = lax.rem(tm + pick(ORDER, phase) + N_TM, N_TM)

        @pl.when(phase == 0)
        def _():
            part = xs.at[pl.ds(LAGS, (N_PIX - 1) * READ)]
            pltpu.make_async_copy(part, part, recv_sem.at[seg]).wait()

        @pl.when(phase > 0)
        def _():
            part = xs.at[pl.ds(LAGS, N_PIX * READ)]
            pltpu.make_async_copy(part, part, recv_sem.at[seg]).wait()

        joined = (pick([before_done(i, -1) for i in range(N_TM)], phase) > 0) & (seg > 0)
        for level, (buf, deeper) in enumerate(((xs, s1), (s1, s2), (s2, s3), (s3, None))):
            level_pass(level, buf, deeper, seg, joined)
        after = lax.rem(seg + 1, N_TM)

        @pl.when((pick([before_done(i, 1) for i in range(N_TM)], phase) > 0) & (after > 0))
        def _():
            border(after)

        return carry

    lax.fori_loop(0, N_TM, segment, 0)

    total = s3[LAGS]
    for i in range(1, FRAMES >> 3):
        total = total + s3[LAGS + i]
    ends[0] = total / (FRAMES >> 3)
    ends[1] = consts[2]

    sent = xs.at[pl.ds(LAGS, (N_DEV - 1) * READ)]
    pltpu.make_async_copy(sent, sent, send_sem).wait()


def finish_kernel(sums, ends, g2_out, mean_out, rows):
    mean, keeper = ends[0], ends[1]
    scale = keeper / (mean * mean)
    mean_out[...] = mean * keeper
    for level in range(LEVELS):
        for half in range(2):
            slot = level * 2 + half
            for k in range(8):
                lag = half * 8 + k
                rows[slot, pl.ds(k * 8, 8), :] = sums[level, lag] * (scale * (1.0 / ((FRAMES >> level) - lag - 1)))
    for level in range(LEVELS):
        for half in range(2):
            for j in range(8):
                g2_out[level, pl.ds(half * 8, 8), pl.ds(j * BLK, BLK)] = rows[level * 2 + half, pl.ds(j, 8, stride=8), :]


def body(raw_frames, frame_order, owner_map, pixel_mask, dark, flat, polarization, solid_angle):
    n_blocks = owner_map.shape[0]
    tiles = [a.reshape(n_blocks, BLK) for a in (dark, flat, polarization, solid_angle, pixel_mask)]
    hbm = pl.BlockSpec(memory_space=pl.ANY)
    vmem = pl.BlockSpec(memory_space=pltpu.VMEM)
    f32 = jnp.float32
    blocks = raw_frames.reshape(READ, n_blocks, BLK).transpose(1, 0, 2)
    sums, ends = pl.pallas_call(
        kernel,
        out_shape=(
            jax.ShapeDtypeStruct((LEVELS, LAGS, 8, BLK), f32),
            jax.ShapeDtypeStruct((2, 8, BLK), f32),
        ),
        in_specs=[hbm] * 8,
        out_specs=(vmem, vmem),
        scratch_shapes=[
            pltpu.VMEM(blocks.shape, f32),
            pltpu.VMEM((GROUP, 8, 8, BLK), f32),
            pltpu.VMEM((N_DEV, READ, 8, BLK), f32),
            pltpu.VMEM((LAGS + FRAMES, 8, BLK), f32),
            pltpu.VMEM((LAGS + FRAMES // 2, 8, BLK), f32),
            pltpu.VMEM((LAGS + FRAMES // 4, 8, BLK), f32),
            pltpu.VMEM((LAGS + FRAMES // 8, 8, BLK), f32),
            pltpu.VMEM((3, 8, BLK), f32),
        ]
        + [pltpu.VMEM((n_blocks, BLK), f32)] * 4
        + [
            pltpu.VMEM((n_blocks, BLK), jnp.int32),
            pltpu.SMEM(owner_map.shape, jnp.int32),
            pltpu.SMEM(frame_order.shape, jnp.int32),
            pltpu.SemaphoreType.DMA,
            pltpu.SemaphoreType.DMA((2,)),
            pltpu.SemaphoreType.DMA((5,)),
            pltpu.SemaphoreType.DMA,
            pltpu.SemaphoreType.DMA,
            pltpu.SemaphoreType.DMA((N_TM,)),
        ],
        compiler_params=pltpu.CompilerParams(collective_id=0, has_side_effects=True),
    )(owner_map, frame_order, blocks, *tiles)
    g2, mean = pl.pallas_call(
        finish_kernel,
        out_shape=(
            jax.ShapeDtypeStruct((LEVELS, LAGS, 8 * BLK), f32),
            jax.ShapeDtypeStruct((8, BLK), f32),
        ),
        in_specs=[vmem, vmem],
        out_specs=(vmem, vmem),
        scratch_shapes=[pltpu.VMEM((2 * LEVELS, 64, BLK), f32)],
    )(sums, ends)
    return g2, mean.reshape(8 * BLK)


def solution(mesh):
    return jax.shard_map(
        body,
        mesh=mesh,
        in_specs=(P(("tm", "pix"), None), P(("tm", "pix")), P(), P(), P(), P(), P(), P()),
        out_specs=(P(None, None, ("pix", "tm")), P(("pix", "tm"))),
        check_vma=False,
    )
```
